32 devices in a mesh: lat: 8 (over y, x, core), lon: 4 (over z).
Axes of the slice: x: 2, y: 2, z: 4, core: 2. Of those that a mesh axis runs over, the one named last changes fastest.
Arguments:
- queries: bfloat16 [8, 8, 64, 1024], P('lat', 'lon'), may hold values from -36 to 36
- keys_values: bfloat16 [2, 8, 8, 64, 1024], P(None, 'lat', 'lon'), may hold values from -4 to 4
- cotangent: bfloat16 [8, 8, 64, 1024], P('lat', 'lon'), may hold values from -6 to 6
- blocks: int32 [8, 8, 6], P('lat', 'lon'), may hold values from 0 to 63, as said below
Outputs:
- attended: bfloat16 [8, 8, 64, 1024], P('lat', 'lon')
- grad_queries: bfloat16 [8, 8, 64, 1024], P('lat', 'lon')
- grad_keys_values: bfloat16 [2, 8, 8, 64, 1024], P(None, 'lat', 'lon')
The draws below stay inside these ranges and needn't reach their ends.
Inputs may be any that keep to these rules, and one draw needn't show every extreme that they name: Entry 0 of each query block's list is the block itself. The other 5 entries are distinct blocks other than itself, whose band differs by at most one from the query block's band and whose sector differs by at most one, counted cyclically over 8 sectors.
All inputs are finite; a program needn't handle non-finite values.
Results may differ from the reference program's by a relative error of at most 0.0085.
Values may be sent and summed in bfloat16 or wider, within the bound.
No kernel may reach another device: no remote copies, remote signals or barrier semaphores. Data moves between devices by JAX's collectives and lax.ppermute only.
A program may use at most 128 MiB of HBM per device.

```python
import jax
import jax.numpy as jnp
from jax import lax

HEADS = 16
HEAD_DIM = 64
D = 1024
CELLS = 64
SAMPLES = 6
GLAT = 8
GLON = 8


def key_field(key):
    base = jax.random.fold_in(key, 11)
    return jnp.clip(jax.random.normal(base, (GLAT, GLON, CELLS, D), jnp.float32), -4.0, 4.0)


def draw_keys_values(key, part):
    keys = key_field(key)
    other = jax.random.fold_in(key, 12)
    values = jnp.clip(jax.random.normal(other, (GLAT, GLON, CELLS, D), jnp.float32), -4.0, 4.0)
    return jnp.stack([keys, values]).astype(jnp.bfloat16)


def draw_queries(key, part):
    other = jax.random.fold_in(key, 13)
    queries = jnp.clip(jax.random.normal(other, (GLAT, GLON, CELLS, D), jnp.float32), -4.0, 4.0)
    return queries.astype(jnp.bfloat16)


def draw_blocks(key, part):
    band_ids = jnp.arange(GLAT, dtype=jnp.int32).reshape(GLAT, 1, 1)
    sector_ids = jnp.arange(GLON, dtype=jnp.int32).reshape(1, GLON, 1)
    shifts = jnp.arange(9, dtype=jnp.int32)
    target_band = band_ids + shifts // 3 - 1
    target_sector = (sector_ids + shifts % 3 - 1) % GLON
    noise = jax.random.randint(key, (GLAT, GLON, 9), 0, 1 << 20)
    invalid = (target_band < 0) | (target_band >= GLAT) | (shifts == 4)
    ranking = noise * 16 + shifts + jnp.where(invalid, 1 << 26, 0)
    picked = jnp.argsort(ranking, axis=-1, stable=True)[:, :, :SAMPLES - 1]
    targets = target_band * GLON + target_sector
    chosen = jnp.take_along_axis(targets, picked, axis=-1)
    itself = jnp.broadcast_to(band_ids * GLON + sector_ids, (GLAT, GLON, 1))
    return jnp.concatenate([itself, chosen], axis=-1).astype(jnp.int32)


def levels(key, shape, cuts, low, top_value):
    def one(axis_at, shards_of):
        heights = jax.random.uniform(jax.random.fold_in(jax.random.fold_in(key, 6), axis_at), (shards_of,), jnp.float32, low / len(cuts), top_value / len(cuts))
        return jnp.repeat(jnp.exp(heights), shape[axis_at] // shards_of).reshape((-1,) + (1,) * (len(shape) - axis_at - 1))

    gain = one(*cuts[0])
    for cut in cuts[1:]:
        gain = gain * one(*cut)
    return gain


def bell_draw(own_key, extent, scale, bound, pieces=(), kind=jnp.bfloat16):
    array = jax.random.normal(own_key, extent, jnp.float32) * scale
    if len(pieces) > 0:
        array = levels(own_key, extent, pieces, -0.22, 0.18) * array
    return jnp.clip(array, min=-bound, max=bound).astype(kind)


def setup_inputs(seed: int = 0) -> dict:
    seeds = jax.random.split(jax.random.key(seed), 5)
    queries = draw_queries(jax.random.fold_in(seeds[4], 71), 0)
    keys_values = draw_keys_values(jax.random.fold_in(seeds[4], 71), 0)
    cotangent = bell_draw(seeds[2], (GLAT, GLON, CELLS, D), 1.0, 6.0, ((0, 8), (1, 4)))
    blocks = draw_blocks(jax.random.fold_in(seeds[4], 71), 0)
    return dict(queries=queries, keys_values=keys_values, cotangent=cotangent, blocks=blocks)


def attend(query, key_sel, value_sel, upstream):
    scale = HEAD_DIM ** -0.5
    query_heads = query.astype(jnp.float32).reshape(CELLS, HEADS, HEAD_DIM)
    key_heads = key_sel.astype(jnp.float32).reshape(SAMPLES * CELLS, HEADS, HEAD_DIM)
    value_heads = value_sel.astype(jnp.float32).reshape(SAMPLES * CELLS, HEADS, HEAD_DIM)
    upstream_heads = upstream.astype(jnp.float32).reshape(CELLS, HEADS, HEAD_DIM)
    scores = jnp.einsum("ihe,jhe->hij", query_heads, key_heads) * scale
    highest = jnp.max(scores, axis=2, keepdims=True)
    raised = jnp.exp(scores - highest)
    weights = raised / jnp.sum(raised, axis=2, keepdims=True)
    weights_low = weights.astype(jnp.bfloat16)
    attended = jnp.einsum("hij,jhe->ihe", weights_low.astype(jnp.float32), value_heads)
    attended = attended.reshape(CELLS, D).astype(jnp.bfloat16)
    pressure = jnp.einsum("ihe,jhe->hij", upstream_heads, value_heads)
    inner = jnp.sum(weights * pressure, axis=2, keepdims=True)
    score_grad = (weights * (pressure - inner) * scale).astype(jnp.bfloat16)
    grad_query = jnp.einsum("hij,jhe->ihe", score_grad.astype(jnp.float32), key_heads)
    grad_query = grad_query.reshape(CELLS, D).astype(jnp.bfloat16)
    grad_key = jnp.einsum("hij,ihe->jhe", score_grad.astype(jnp.float32), query_heads).reshape(SAMPLES, CELLS, D)
    grad_value = jnp.einsum("hij,ihe->jhe", weights_low.astype(jnp.float32), upstream_heads).reshape(SAMPLES, CELLS, D)
    return attended, grad_query, grad_key, grad_value


def reference(queries, keys_values, cotangent, blocks):
    count = GLAT * GLON
    query_flat = queries.reshape(count, CELLS, D)
    key_flat = keys_values[0].reshape(count, CELLS, D)
    value_flat = keys_values[1].reshape(count, CELLS, D)
    upstream_flat = cotangent.reshape(count, CELLS, D)
    list_flat = blocks.reshape(count, SAMPLES).astype(jnp.int32)

    def step(carry, item):
        query, upstream, chosen = item
        attended, grad_query, grad_key, grad_value = attend(query, key_flat[chosen], value_flat[chosen], upstream)
        carry = carry.at[0, chosen].add(grad_key)
        carry = carry.at[1, chosen].add(grad_value)
        return carry, (attended, grad_query)

    zeros = jnp.zeros((2, count, CELLS, D), jnp.float32)
    grads, outputs = lax.scan(step, zeros, (query_flat, upstream_flat, list_flat))
    attended = outputs[0].reshape(GLAT, GLON, CELLS, D)
    grad_queries = outputs[1].reshape(GLAT, GLON, CELLS, D)
    grad_keys_values = grads.reshape(2, GLAT, GLON, CELLS, D).astype(jnp.bfloat16)
    return (attended, grad_queries, grad_keys_values)
```

```python
import jax
import jax.numpy as jnp
from jax import lax
from jax.experimental import pallas as pl
from jax.experimental.pallas import tpu as pltpu
from jax.sharding import PartitionSpec as P

HEAD_DIM = 64
GROUP = 4
LANES = GROUP * HEAD_DIM
LOG2E = 1.4426950408889634


def lon_shift(value, steps):
    count = lax.axis_size("lon")
    return lax.ppermute(value, "lon", [(i, (i + steps) % count) for i in range(count)])


def intra_swap(value):
    count = lax.axis_size("lat")
    return lax.ppermute(value, "lat", [(i, i ^ 1) for i in range(count) if i ^ 1 < count])


def inter_swap(value):
    count = lax.axis_size("lat")
    pairs = [(i, i + 1 if i % 2 else i - 1) for i in range(count)]
    return lax.ppermute(value, "lat", [(i, j) for i, j in pairs if 0 <= j < count])


def dot(a, b, dims):
    return lax.dot_general(a, b, (dims, ((), ())), preferred_element_type=jnp.float32)


def attention_kernel(
    slots,
    q_ref,
    c_ref,
    own_ref,
    intra_ref,
    inter_ref,
    west_ref,
    east_ref,
    side_ref,
    xk_ref,
    xwv_ref,
    xev_ref,
    att_ref,
    gq_ref,
    gown_ref,
    gside_ref,
    gintra_ref,
    ginter_ref,
    gxk_ref,
    gxwv_ref,
    gxev_ref,
    kv,
    grad,
):
    cols = q_ref.shape[1]
    cells = q_ref.shape[2]
    wide = cols + 2
    samples = slots.shape[1]
    scale = HEAD_DIM**-0.5
    for part in range(2):
        for c in range(cols):
            kv[part, c] = own_ref[part, 0, c]
            kv[part, wide + c] = intra_ref[part, 0, c]
            kv[part, 2 * wide + c] = inter_ref[part, 0, c]
        kv[part, cols] = west_ref[part, 0, 0]
        kv[part, cols + 1] = east_ref[part, 0, 0]
        kv[part, wide + cols] = side_ref[part, 0, 0]
        kv[part, wide + cols + 1] = side_ref[part, 0, 1]
    kv[0, 2 * wide + cols] = xk_ref[0, 0, 0]
    kv[0, 2 * wide + cols + 1] = xk_ref[0, 0, 1]
    kv[1, 2 * wide + cols] = xwv_ref[0, 0, 0]
    kv[1, 2 * wide + cols + 1] = xev_ref[0, 0, 0]
    grad[...] = jnp.zeros_like(grad)

    head = lax.broadcasted_iota(jnp.int32, (cells, LANES), 1) // HEAD_DIM
    masks = [head == h for h in range(GROUP)]

    def spread(rows):
        zero = jnp.zeros_like(rows)
        return jnp.concatenate([jnp.where(m, rows, zero) for m in masks], axis=0)

    def gathered(rows):
        out = rows[:cells]
        for h in range(1, GROUP):
            out = jnp.where(masks[h], rows[h * cells : (h + 1) * cells], out)
        return out

    for b in range(cols):
        listed = [slots[b, s] for s in range(samples)]
        query = spread(q_ref[0, b])
        upstream = spread(c_ref[0, b])
        keys = jnp.concatenate([kv[0, s] for s in listed], axis=0)
        values = jnp.concatenate([kv[1, s] for s in listed], axis=0)
        scores = dot(keys, query, ((1,), (1,)))
        highest = jnp.max(scores, axis=0, keepdims=True)
        raised = jnp.exp2((scores - highest) * (scale * LOG2E))
        weights = raised * (1.0 / jnp.sum(raised, axis=0, keepdims=True))
        low = weights.astype(jnp.bfloat16)
        pressure = dot(values, upstream, ((1,), (1,)))
        inner = jnp.sum(weights * pressure, axis=0, keepdims=True)
        score_grad = (weights * (pressure - inner) * scale).astype(jnp.bfloat16)
        att_ref[0, b] = gathered(dot(low, values, ((0,), (0,)))).astype(att_ref.dtype)
        gq_ref[0, b] = gathered(dot(score_grad, keys, ((0,), (0,)))).astype(gq_ref.dtype)
        grad_keys = dot(score_grad, query, ((1,), (0,)))
        grad_values = dot(low, upstream, ((1,), (0,)))
        for s in range(samples):
            grad[0, listed[s]] += grad_keys[s * cells : (s + 1) * cells]
            grad[1, listed[s]] += grad_values[s * cells : (s + 1) * cells]

    for part in range(2):
        for c in range(cols):
            gown_ref[part, 0, c] = grad[part, c]
            ginter_ref[part, 0, c] = grad[part, 2 * wide + c]
        for c in range(wide):
            gintra_ref[part, 0, c] = grad[part, wide + c].astype(gintra_ref.dtype)
        for side in range(2):
            gside_ref[part, 0, side] = grad[part, cols + side]
    for side in range(2):
        gxk_ref[0, 0, side] = grad[0, 2 * wide + cols + side].astype(gxk_ref.dtype)
    gxwv_ref[0, 0, 0] = grad[1, 2 * wide + cols].astype(gxwv_ref.dtype)
    gxev_ref[0, 0, 0] = grad[1, 2 * wide + cols + 1].astype(gxev_ref.dtype)


def attention(slots, operands):
    queries = operands[0]
    _, cols, cells, width = queries.shape
    wide = cols + 2

    def spec(shape):
        block = tuple(shape[:-1]) + (LANES,)
        lead = (0,) * (len(shape) - 1)
        return pl.BlockSpec(block, lambda g, s: lead + (g,))

    def out(lead, dtype):
        return jax.ShapeDtypeStruct(lead + (cells, width), dtype)

    low, full = jnp.bfloat16, jnp.float32
    outs = [
        out((1, cols), low),
        out((1, cols), low),
        out((2, 1, cols), full),
        out((2, 1, 2), full),
        out((2, 1, wide), low),
        out((2, 1, cols), full),
        out((1, 1, 2), low),
        out((1, 1, 1), low),
        out((1, 1, 1), low),
    ]
    keys = slots.shape[1] * cells
    flops = 2 * 6 * cols * width * GROUP * cells * keys
    moved = sum(x.size * x.dtype.itemsize for x in list(operands) + outs)
    return pl.pallas_call(
        attention_kernel,
        out_shape=outs,
        grid_spec=pltpu.PrefetchScalarGridSpec(
            num_scalar_prefetch=1,
            grid=(width // LANES,),
            in_specs=[spec(x.shape) for x in operands],
            out_specs=[spec(x.shape) for x in outs],
            scratch_shapes=[
                pltpu.VMEM((2, 3 * wide, cells, LANES), low),
                pltpu.VMEM((2, 3 * wide, cells, LANES), full),
            ],
        ),
        cost_estimate=pl.CostEstimate(
            flops=flops, bytes_accessed=moved, transcendentals=cols * width * keys
        ),
        name="attention",
    )(slots, *operands)


def block_slots(blocks, cols):
    sectors = cols * lax.axis_size("lon")
    lat, lon = lax.axis_index("lat"), lax.axis_index("lon")
    down = blocks // sectors - lat
    near = jnp.where(lat % 2 == 0, 1, -1)
    row = jnp.where(down == 0, 0, jnp.where(down == near, 1, 2))
    place = (blocks % sectors - lon * cols + 1) % sectors
    col = jnp.where(place == 0, cols, jnp.where(place <= cols, place - 1, cols + 1))
    return row * (cols + 2) + col


def body(queries, keys_values, cotangent, blocks):
    cols = queries.shape[1]
    slots = block_slots(blocks[0], cols)

    inter = inter_swap(keys_values)
    west = lon_shift(keys_values[:, :, cols - 1 :], 1)
    east = lon_shift(keys_values[:, :, :1], -1)
    intra = intra_swap(keys_values)
    west_values = lon_shift(inter[1:, :, cols - 1 :], 1)
    east_values = lon_shift(inter[1:, :, :1], -1)
    sides = jnp.concatenate([west, east], axis=2)
    corner_keys = inter_swap(sides[:1])
    intra_sides = intra_swap(sides)

    operands = (
        queries,
        cotangent,
        keys_values,
        intra,
        inter,
        west,
        east,
        intra_sides,
        corner_keys,
        west_values,
        east_values,
    )
    attended, grad_queries, own, side, to_intra, to_inter, to_xk, to_xwv, to_xev = attention(
        slots, operands
    )

    low, full = jnp.bfloat16, jnp.float32
    from_xk = inter_swap(to_xk).astype(full)
    from_xwv = lon_shift(to_xwv, -1).astype(full)
    from_xev = lon_shift(to_xev, 1).astype(full)
    from_intra = intra_swap(to_intra).astype(full)
    side = side + from_intra[:, :, cols:]
    side = jnp.concatenate([side[:1] + from_xk, side[1:]], axis=0).astype(low)
    from_east = lon_shift(side[:, :, :1], -1).astype(full)
    from_west = lon_shift(side[:, :, 1:], 1).astype(full)
    to_inter = to_inter.at[1:, :, cols - 1 :].add(from_xwv).at[1:, :, :1].add(from_xev)
    from_inter = inter_swap(to_inter.astype(low)).astype(full)
    own = own + from_intra[:, :, :cols] + from_inter
    own = own.at[:, :, cols - 1 :].add(from_east).at[:, :, :1].add(from_west)
    return (attended, grad_queries, own.astype(low))


def solution(mesh):
    placed = (
        P("lat", "lon", None, None),
        P(None, "lat", "lon", None, None),
        P("lat", "lon", None, None),
        P("lat", "lon", None),
    )
    return jax.shard_map(
        body,
        mesh=mesh,
        in_specs=placed,
        out_specs=(placed[0], placed[0], placed[1]),
        check_vma=False,
    )
```

```python
import jax
import jax.numpy as jnp
from jax import lax
from jax.experimental import pallas as pl
from jax.experimental.pallas import tpu as pltpu
from jax.sharding import PartitionSpec as P

HEAD_DIM = 64
GROUP = 4
LANES = GROUP * HEAD_DIM
LOG2E = 1.4426950408889634


def lon_shift(value, steps):
    count = lax.axis_size("lon")
    return lax.ppermute(value, "lon", [(i, (i + steps) % count) for i in range(count)])


def intra_swap(value):
    count = lax.axis_size("lat")
    return lax.ppermute(value, "lat", [(i, i ^ 1) for i in range(count) if i ^ 1 < count])


def inter_swap(value):
    count = lax.axis_size("lat")
    pairs = [(i, i + 1 if i % 2 else i - 1) for i in range(count)]
    return lax.ppermute(value, "lat", [(i, j) for i, j in pairs if 0 <= j < count])


def dot(a, b, dims):
    return lax.dot_general(a, b, (dims, ((), ())), preferred_element_type=jnp.float32)


def attention_kernel(
    slots,
    q_ref,
    c_ref,
    own_ref,
    intra_ref,
    inter_ref,
    west_ref,
    east_ref,
    side_ref,
    xk_ref,
    xwv_ref,
    xev_ref,
    att_ref,
    gq_ref,
    gown_ref,
    gside_ref,
    gintra_ref,
    gnk_ref,
    gnv_ref,
    gxk_ref,
    gxwv_ref,
    gxev_ref,
    kv,
    grad,
):
    cols = q_ref.shape[1]
    cells = q_ref.shape[2]
    wide = cols + 2
    samples = slots.shape[1]
    scale = HEAD_DIM**-0.5
    for part in range(2):
        for c in range(cols):
            kv[part, c] = own_ref[part, 0, c]
            kv[part, wide + c] = intra_ref[part, 0, c]
            kv[part, 2 * wide + c] = inter_ref[part, 0, c]
        kv[part, cols] = west_ref[part, 0, 0]
        kv[part, cols + 1] = east_ref[part, 0, 0]
        kv[part, wide + cols] = side_ref[part, 0, 0]
        kv[part, wide + cols + 1] = side_ref[part, 0, 1]
    kv[0, 2 * wide + cols] = xk_ref[0, 0, 0]
    kv[0, 2 * wide + cols + 1] = xk_ref[0, 0, 1]
    kv[1, 2 * wide + cols] = xwv_ref[0, 0, 0]
    kv[1, 2 * wide + cols + 1] = xev_ref[0, 0, 0]
    grad[...] = jnp.zeros_like(grad)

    head = lax.broadcasted_iota(jnp.int32, (cells, LANES), 1) // HEAD_DIM
    masks = [head == h for h in range(GROUP)]

    def spread(rows):
        zero = jnp.zeros_like(rows)
        return jnp.concatenate([jnp.where(m, rows, zero) for m in masks], axis=0)

    def gathered(rows):
        out = rows[:cells]
        for h in range(1, GROUP):
            out = jnp.where(masks[h], rows[h * cells : (h + 1) * cells], out)
        return out

    for b in range(cols):
        listed = [slots[b, s] for s in range(samples)]
        query = spread(q_ref[0, b])
        upstream = spread(c_ref[0, b])
        keys = jnp.concatenate([kv[0, s] for s in listed], axis=0)
        values = jnp.concatenate([kv[1, s] for s in listed], axis=0)
        scores = dot(keys, query, ((1,), (1,)))
        highest = jnp.max(scores, axis=0, keepdims=True)
        raised = jnp.exp2((scores - highest) * (scale * LOG2E))
        weights = raised * (1.0 / jnp.sum(raised, axis=0, keepdims=True))
        low = weights.astype(jnp.bfloat16)
        pressure = dot(values, upstream, ((1,), (1,)))
        inner = jnp.sum(weights * pressure, axis=0, keepdims=True)
        score_grad = (weights * (pressure - inner) * scale).astype(jnp.bfloat16)
        att_ref[0, b] = gathered(dot(low, values, ((0,), (0,)))).astype(att_ref.dtype)
        gq_ref[0, b] = gathered(dot(score_grad, keys, ((0,), (0,)))).astype(gq_ref.dtype)
        grad_keys = dot(score_grad, query, ((1,), (0,)))
        grad_values = dot(low, upstream, ((1,), (0,)))
        for s in range(samples):
            grad[0, listed[s]] += grad_keys[s * cells : (s + 1) * cells]
            grad[1, listed[s]] += grad_values[s * cells : (s + 1) * cells]

    for c in range(cols):
        gnk_ref[0, 0, c] = grad[0, 2 * wide + c].astype(gnk_ref.dtype)
        gnv_ref[0, 0, c] = grad[1, 2 * wide + c]
    for part in range(2):
        for c in range(cols):
            gown_ref[part, 0, c] = grad[part, c]
        for c in range(wide):
            gintra_ref[part, 0, c] = grad[part, wide + c].astype(gintra_ref.dtype)
        for side in range(2):
            gside_ref[part, 0, side] = grad[part, cols + side]
    for side in range(2):
        gxk_ref[0, 0, side] = grad[0, 2 * wide + cols + side].astype(gxk_ref.dtype)
    gxwv_ref[0, 0, 0] = grad[1, 2 * wide + cols].astype(gxwv_ref.dtype)
    gxev_ref[0, 0, 0] = grad[1, 2 * wide + cols + 1].astype(gxev_ref.dtype)


def attention(slots, operands):
    queries = operands[0]
    _, cols, cells, width = queries.shape
    wide = cols + 2

    def spec(shape):
        block = tuple(shape[:-1]) + (LANES,)
        lead = (0,) * (len(shape) - 1)
        return pl.BlockSpec(block, lambda g, s: lead + (g,))

    def out(lead, dtype):
        return jax.ShapeDtypeStruct(lead + (cells, width), dtype)

    low, full = jnp.bfloat16, jnp.float32
    outs = [
        out((1, cols), low),
        out((1, cols), low),
        out((2, 1, cols), full),
        out((2, 1, 2), full),
        out((2, 1, wide), low),
        out((1, 1, cols), low),
        out((1, 1, cols), full),
        out((1, 1, 2), low),
        out((1, 1, 1), low),
        out((1, 1, 1), low),
    ]
    keys = slots.shape[1] * cells
    flops = 2 * 6 * cols * width * GROUP * cells * keys
    moved = sum(x.size * x.dtype.itemsize for x in list(operands) + outs)
    return pl.pallas_call(
        attention_kernel,
        out_shape=outs,
        grid_spec=pltpu.PrefetchScalarGridSpec(
            num_scalar_prefetch=1,
            grid=(width // LANES,),
            in_specs=[spec(x.shape) for x in operands],
            out_specs=[spec(x.shape) for x in outs],
            scratch_shapes=[
                pltpu.VMEM((2, 3 * wide, cells, LANES), low),
                pltpu.VMEM((2, 3 * wide, cells, LANES), full),
            ],
        ),
        cost_estimate=pl.CostEstimate(
            flops=flops, bytes_accessed=moved, transcendentals=cols * width * keys
        ),
        compiler_params=pltpu.CompilerParams(vmem_limit_bytes=67043328),
        name="attention",
    )(slots, *operands)


def block_slots(blocks, cols):
    sectors = cols * lax.axis_size("lon")
    lat, lon = lax.axis_index("lat"), lax.axis_index("lon")
    down = blocks // sectors - lat
    near = jnp.where(lat % 2 == 0, 1, -1)
    row = jnp.where(down == 0, 0, jnp.where(down == near, 1, 2))
    place = (blocks % sectors - lon * cols + 1) % sectors
    col = jnp.where(place == 0, cols, jnp.where(place <= cols, place - 1, cols + 1))
    return row * (cols + 2) + col


def edges(first, last, cols):
    still = ((0, 0, 0),)
    return lax.pad(first, jnp.zeros((), first.dtype), still * 2 + ((0, cols - 1, 0),) + still * 2) + lax.pad(
        last, jnp.zeros((), last.dtype), still * 2 + ((cols - 1, 0, 0),) + still * 2
    )


def named(scope, move, *args):
    with jax.named_scope(scope):
        return move(*args)


def body(queries, keys_values, cotangent, blocks):
    cols = queries.shape[1]
    slots = block_slots(blocks[0], cols)

    west = named("in_west", lon_shift, keys_values[:, :, cols - 1 :], 1)
    east = named("in_east", lon_shift, keys_values[:, :, :1], -1)
    inter = named("in_inter", inter_swap, keys_values)
    intra = named("in_intra", intra_swap, keys_values)
    sides = jnp.concatenate([west, east], axis=2)
    intra_sides = named("in_side", intra_swap, sides)
    corner_keys = named("in_xk", inter_swap, sides[:1])
    west_values = named("in_xwv", lon_shift, inter[1:, :, cols - 1 :], 1)
    east_values = named("in_xev", lon_shift, inter[1:, :, :1], -1)

    operands = (
        queries,
        cotangent,
        keys_values,
        intra,
        inter,
        west,
        east,
        intra_sides,
        corner_keys,
        west_values,
        east_values,
    )
    outs = attention(slots, operands)
    attended, grad_queries, own, side, to_intra, near_k, near_v, to_xk, to_xwv, to_xev = outs

    low, full = jnp.bfloat16, jnp.float32
    from_xk = named("out_xk", inter_swap, to_xk).astype(full)
    from_xwv = named("out_xwv", lon_shift, to_xwv, -1).astype(full)
    from_xev = named("out_xev", lon_shift, to_xev, 1).astype(full)
    from_intra = named("out_intra", intra_swap, to_intra).astype(full)
    side = side + from_intra[:, :, cols:]
    side_k, side_v = (side[:1] + from_xk).astype(low), side[1:].astype(low)
    from_east = named(
        "out_east", lon_shift, jnp.concatenate([side_k[:, :, :1], side_v[:, :, :1]], axis=0), -1
    )
    from_west = named(
        "out_west", lon_shift, jnp.concatenate([side_k[:, :, 1:], side_v[:, :, 1:]], axis=0), 1
    )
    near_v = (near_v + edges(from_xev, from_xwv, cols)).astype(low)
    from_inter = named("out_inter", inter_swap, jnp.concatenate([near_k, near_v], axis=0))
    own = own + from_intra[:, :, :cols] + from_inter.astype(full)
    own = own + edges(from_west.astype(full), from_east.astype(full), cols)
    return (attended, grad_queries, own.astype(low))


def solution(mesh):
    placed = (
        P("lat", "lon", None, None),
        P(None, "lat", "lon", None, None),
        P("lat", "lon", None, None),
        P("lat", "lon", None),
    )
    return jax.shard_map(
        body,
        mesh=mesh,
        in_specs=placed,
        out_specs=(placed[0], placed[0], placed[1]),
        check_vma=False,
    )
```

```python
import jax
import jax.numpy as jnp
from jax import lax
from jax.experimental import pallas as pl
from jax.experimental.pallas import tpu as pltpu
from jax.sharding import PartitionSpec as P


HEAD_DIM = 64
GROUP = 4
LANES = GROUP * HEAD_DIM
LOG2E = 1.4426950408889634


def lon_shift(value, steps):
    count = lax.axis_size("lon")
    return lax.ppermute(value, "lon", [(i, (i + steps) % count) for i in range(count)])


def intra_swap(value):
    count = lax.axis_size("lat")
    return lax.ppermute(value, "lat", [(i, i ^ 1) for i in range(count) if i ^ 1 < count])


def inter_swap(value):
    count = lax.axis_size("lat")
    pairs = [(i, i + 1 if i % 2 else i - 1) for i in range(count)]
    return lax.ppermute(value, "lat", [(i, j) for i, j in pairs if 0 <= j < count])


def dot(a, b, dims):
    return lax.dot_general(a, b, (dims, ((), ())), preferred_element_type=jnp.float32)


def attention_kernel(
    slots,
    places,
    q_ref,
    c_ref,
    own_ref,
    intra_ref,
    ik_ref,
    iv_ref,
    wk_ref,
    ek_ref,
    wv_ref,
    ev_ref,
    sk_ref,
    sw_ref,
    se_ref,
    ck_ref,
    cw_ref,
    ce_ref,
    att_ref,
    gq_ref,
    gown_ref,
    gsk_ref,
    gsv_ref,
    gintra_ref,
    gik_ref,
    giv_ref,
    gck_ref,
    gcw_ref,
    gce_ref,
    kv,
    grad,
    sems,
):
    _, cols, cells, width = q_ref.shape
    wide = cols + 2
    samples = slots.shape[1]
    groups = width // LANES
    scale = HEAD_DIM**-0.5
    low = jnp.bfloat16

    near, far = pl.ds(0, cols), pl.ds(2 * wide, cols)
    moves = (
        (own_ref, slice(None), 0, near),
        (intra_ref, slice(None), 0, pl.ds(wide, cols)),
        (ik_ref, pl.ds(0, 1), 0, far),
        (iv_ref, pl.ds(1, 1), 0, far),
        (wk_ref, pl.ds(0, 1), 0, pl.ds(cols, 1)),
        (ek_ref, pl.ds(0, 1), 0, pl.ds(cols + 1, 1)),
        (wv_ref, pl.ds(1, 1), 0, pl.ds(cols, 1)),
        (ev_ref, pl.ds(1, 1), 0, pl.ds(cols + 1, 1)),
        (sk_ref, pl.ds(0, 1), 0, pl.ds(wide + cols, 2)),
        (sw_ref, pl.ds(1, 1), 0, pl.ds(wide + cols, 1)),
        (se_ref, pl.ds(1, 1), 0, pl.ds(wide + cols + 1, 1)),
        (ck_ref, pl.ds(0, 1), 0, pl.ds(2 * wide + cols, 2)),
        (cw_ref, pl.ds(1, 1), 0, pl.ds(2 * wide + cols, 1)),
        (ce_ref, pl.ds(1, 1), 0, pl.ds(2 * wide + cols + 1, 1)),
    )

    def copies(g):
        lanes = pl.ds(0, LANES) if g == 0 else pl.ds(LANES, width - LANES)
        return [
            pltpu.make_async_copy(
                ref.at[:, row, :, :, lanes], kv.at[part, place, :, lanes], sems.at[g, i]
            )
            for i, (ref, part, row, place) in enumerate(moves)
        ]

    pieces = range(min(groups, 2))
    for piece in pieces:
        for copy in copies(piece):
            copy.start()
    for b in range(cols):
        for part in range(2):
            grad[b, part, samples] = jnp.zeros((cells, LANES), jnp.float32)

    head = lax.broadcasted_iota(jnp.int32, (cells, LANES), 1) // HEAD_DIM
    masks = [head == h for h in range(GROUP)]

    def spread(rows):
        zero = jnp.zeros_like(rows)
        return jnp.concatenate([jnp.where(m, rows, zero) for m in masks], axis=0)

    def gathered(rows):
        out = rows[:cells]
        for h in range(1, GROUP):
            out = jnp.where(masks[h], rows[h * cells : (h + 1) * cells], out)
        return out

    def step(g):
        lanes = pl.ds(g * LANES, LANES)
        if g in pieces:
            for copy in copies(g):
                copy.wait()
        spans = range(cols)
        listed = [[slots[b, s] for s in range(samples)] for b in spans]
        query = [spread(q_ref[0, b, :, lanes]) for b in spans]
        upstream = [spread(c_ref[0, b, :, lanes]) for b in spans]
        keys = [jnp.concatenate([kv[0, s, :, lanes] for s in x], axis=0) for x in listed]
        values = [jnp.concatenate([kv[1, s, :, lanes] for s in x], axis=0) for x in listed]
        scores = [dot(keys[b], query[b], ((1,), (1,))) for b in spans]
        pressure = [dot(values[b], upstream[b], ((1,), (1,))) for b in spans]
        for b in spans:
            highest = jnp.max(scores[b], axis=0, keepdims=True)
            raised = jnp.exp2((scores[b] - highest) * (scale * LOG2E))
            weights = raised * (1.0 / jnp.sum(raised, axis=0, keepdims=True))
            weights_low = weights.astype(low)
            inner = jnp.sum(weights * pressure[b], axis=0, keepdims=True)
            score_grad = (weights * (pressure[b] - inner) * scale).astype(low)
            grad_values = dot(weights_low, upstream[b], ((1,), (0,)))
            grad_keys = dot(score_grad, query[b], ((1,), (0,)))
            att_ref[0, b, :, lanes] = gathered(dot(weights_low, values[b], ((0,), (0,)))).astype(low)
            gq_ref[0, b, :, lanes] = gathered(dot(score_grad, keys[b], ((0,), (0,)))).astype(low)
            for s in range(samples):
                grad[b, 0, s] = grad_keys[s * cells : (s + 1) * cells]
                grad[b, 1, s] = grad_values[s * cells : (s + 1) * cells]

        def merged(part, row, col):
            place = {cols: -1, cols + 1: cols}.get(col, col)
            slot = row * wide + col
            terms = [
                grad[b, part, places[b, slot]] for b in range(cols) if abs(b - place) <= 1
            ]
            return sum(terms[1:], terms[0])

        for c in range(cols):
            gik_ref[0, 0, c, :, lanes] = merged(0, 2, c).astype(low)
            giv_ref[0, 0, c, :, lanes] = merged(1, 2, c)
        for part in range(2):
            for c in range(cols):
                gown_ref[part, 0, c, :, lanes] = merged(part, 0, c)
            for c in range(wide):
                gintra_ref[part, 0, c, :, lanes] = merged(part, 1, c).astype(low)
        for side in range(2):
            gsk_ref[0, 0, side, :, lanes] = merged(0, 0, cols + side)
            gsv_ref[0, 0, side, :, lanes] = merged(1, 0, cols + side)
            gck_ref[0, 0, side, :, lanes] = merged(0, 2, cols + side).astype(low)
        gcw_ref[0, 0, 0, :, lanes] = merged(1, 2, cols).astype(low)
        gce_ref[0, 0, 0, :, lanes] = merged(1, 2, cols + 1).astype(low)

    for g in range(groups):
        step(g)


def attention(slots, places, operands):
    queries = operands[0]
    _, cols, cells, width = queries.shape
    wide = cols + 2
    samples = slots.shape[1]

    def out(lead, dtype):
        return jax.ShapeDtypeStruct(lead + (cells, width), dtype)

    low, full = jnp.bfloat16, jnp.float32
    outs = [
        out((1, cols), low),
        out((1, cols), low),
        out((2, 1, cols), full),
        out((1, 1, 2), full),
        out((1, 1, 2), full),
        out((2, 1, wide), low),
        out((1, 1, cols), low),
        out((1, 1, cols), full),
        out((1, 1, 2), low),
        out((1, 1, 1), low),
        out((1, 1, 1), low),
    ]
    keys = samples * cells
    flops = 2 * 6 * cols * width * GROUP * cells * keys
    moved = sum(x.size * x.dtype.itemsize for x in list(operands) + outs)
    scalar, vector, anywhere = (
        pl.BlockSpec(memory_space=space) for space in (pltpu.SMEM, pltpu.VMEM, pl.ANY)
    )
    return pl.pallas_call(
        attention_kernel,
        out_shape=outs,
        in_specs=[scalar] * 2 + [vector] * 2 + [anywhere] * (len(operands) - 2),
        out_specs=[vector] * len(outs),
        scratch_shapes=[
            pltpu.VMEM((2, 3 * wide, cells, width), low),
            pltpu.VMEM((cols, 2, samples + 1, cells, LANES), full),
            pltpu.SemaphoreType.DMA((2, len(operands) - 2)),
        ],
        cost_estimate=pl.CostEstimate(
            flops=flops, bytes_accessed=moved, transcendentals=cols * width * keys
        ),
        compiler_params=pltpu.CompilerParams(vmem_limit_bytes=20 * 1024 * 1024),
        name="attention",
    )(slots, places, *operands)


def block_slots(blocks, cols):
    sectors = cols * lax.axis_size("lon")
    lat, lon = lax.axis_index("lat"), lax.axis_index("lon")
    down = blocks // sectors - lat
    near = jnp.where(lat % 2 == 0, 1, -1)
    row = jnp.where(down == 0, 0, jnp.where(down == near, 1, 2))
    place = (blocks % sectors - lon * cols + 1) % sectors
    col = jnp.where(place == 0, cols, jnp.where(place <= cols, place - 1, cols + 1))
    slots = row * (cols + 2) + col
    samples = blocks.shape[-1]
    listed = slots[:, :, None] == jnp.arange(3 * (cols + 2), dtype=jnp.int32)
    order = jnp.arange(samples, dtype=jnp.int32)[None, :, None]
    places = samples + jnp.sum(jnp.where(listed, order - samples, 0), axis=1, dtype=jnp.int32)
    return slots, places


def edges(first, last, cols):
    still = ((0, 0, 0),)
    return lax.pad(first, jnp.zeros((), first.dtype), still * 2 + ((0, cols - 1, 0),) + still * 2) + lax.pad(
        last, jnp.zeros((), last.dtype), still * 2 + ((cols - 1, 0, 0),) + still * 2
    )


def body(queries, keys_values, cotangent, blocks):
    cols = queries.shape[1]
    slots, places = block_slots(blocks[0], cols)

    keys, values = keys_values[:1], keys_values[1:]
    west_keys = lon_shift(keys[:, :, cols - 1 :], 1)
    east_keys = lon_shift(keys[:, :, :1], -1)
    inter_values = inter_swap(values)
    west_values = lon_shift(values[:, :, cols - 1 :], 1)
    east_values = lon_shift(values[:, :, :1], -1)
    inter_keys = inter_swap(keys)
    intra = intra_swap(keys_values)
    side_keys = jnp.concatenate([west_keys, east_keys], axis=2)
    corner_keys = inter_swap(side_keys)
    corner_west = lon_shift(inter_values[:, :, cols - 1 :], 1)
    corner_east = lon_shift(inter_values[:, :, :1], -1)
    intra_side_keys = intra_swap(side_keys)
    intra_west = intra_swap(west_values)
    intra_east = intra_swap(east_values)

    operands = (
        queries,
        cotangent,
        keys_values,
        intra,
        inter_keys,
        inter_values,
        west_keys,
        east_keys,
        west_values,
        east_values,
        intra_side_keys,
        intra_west,
        intra_east,
        corner_keys,
        corner_west,
        corner_east,
    )
    outs = attention(slots, places, operands)
    attended, grad_queries, own, side_k, side_v, to_intra, near_k, near_v, far_k, far_w, far_e = outs

    low, full = jnp.bfloat16, jnp.float32
    from_k = inter_swap(far_k)
    from_w = lon_shift(far_w, -1)
    from_e = lon_shift(far_e, 1)
    from_intra = intra_swap(to_intra)
    from_inter_k = inter_swap(near_k)
    side_v = (side_v + from_intra[1:, :, cols:].astype(full)).astype(low)
    from_east_v = lon_shift(side_v[:, :, :1], -1)
    from_west_v = lon_shift(side_v[:, :, 1:], 1)
    side_k = (side_k + from_intra[:1, :, cols:].astype(full) + from_k.astype(full)).astype(low)
    from_east_k = lon_shift(side_k[:, :, :1], -1)
    from_west_k = lon_shift(side_k[:, :, 1:], 1)
    near_v = (near_v + edges(from_e.astype(full), from_w.astype(full), cols)).astype(low)
    from_inter_v = inter_swap(near_v)

    def total(part, inter, first, last):
        piece = own[part : part + 1] + from_intra[part : part + 1, :, :cols].astype(full)
        piece = piece + inter.astype(full) + edges(first.astype(full), last.astype(full), cols)
        return piece.astype(low)

    grads = jnp.concatenate(
        [
            total(0, from_inter_k, from_west_k, from_east_k),
            total(1, from_inter_v, from_west_v, from_east_v),
        ],
        axis=0,
    )
    return (attended, grad_queries, grads)


def solution(mesh):
    placed = (
        P("lat", "lon", None, None),
        P(None, "lat", "lon", None, None),
        P("lat", "lon", None, None),
        P("lat", "lon", None),
    )
    return jax.shard_map(
        body,
        mesh=mesh,
        in_specs=placed,
        out_specs=(placed[0], placed[0], placed[1]),
        check_vma=False,
    )
```

```python
import jax
import jax.numpy as jnp
from jax import lax
from jax.experimental import pallas as pl
from jax.experimental.pallas import tpu as pltpu
from jax.sharding import PartitionSpec as P


HEAD_DIM = 64
GROUP = 4
LANES = GROUP * HEAD_DIM
LOG2E = 1.4426950408889634


def lon_shift(value, steps):
    count = lax.axis_size("lon")
    return lax.ppermute(value, "lon", [(i, (i + steps) % count) for i in range(count)])


def intra_swap(value):
    count = lax.axis_size("lat")
    return lax.ppermute(value, "lat", [(i, i ^ 1) for i in range(count) if i ^ 1 < count])


def inter_swap(value):
    count = lax.axis_size("lat")
    pairs = [(i, i + 1 if i % 2 else i - 1) for i in range(count)]
    return lax.ppermute(value, "lat", [(i, j) for i, j in pairs if 0 <= j < count])


def dot(a, b, dims):
    return lax.dot_general(a, b, (dims, ((), ())), preferred_element_type=jnp.float32)


def attention_kernel(
    slots,
    places,
    q_ref,
    c_ref,
    own_ref,
    intra_ref,
    inter_ref,
    wk_ref,
    ek_ref,
    wv_ref,
    ev_ref,
    sk_ref,
    sw_ref,
    se_ref,
    ck_ref,
    cw_ref,
    ce_ref,
    kv,
    shares,
    gown_ref,
    gsk_ref,
    gsv_ref,
    gintra_ref,
    gik_ref,
    giv_ref,
    gck_ref,
    gcw_ref,
    gce_ref,
    grad,
    sems,
):
    _, cols, cells, width = q_ref.shape
    wide = cols + 2
    samples = slots.shape[1]
    groups = width // LANES
    scale = HEAD_DIM**-0.5
    low = jnp.bfloat16

    near, far = pl.ds(0, cols), pl.ds(2 * wide, cols)
    moves = (
        (own_ref, slice(None), 0, near),
        (intra_ref, slice(None), 0, pl.ds(wide, cols)),
        (inter_ref, slice(None), 0, far),
        (wk_ref, pl.ds(0, 1), 0, pl.ds(cols, 1)),
        (ek_ref, pl.ds(0, 1), 0, pl.ds(cols + 1, 1)),
        (wv_ref, pl.ds(1, 1), 0, pl.ds(cols, 1)),
        (ev_ref, pl.ds(1, 1), 0, pl.ds(cols + 1, 1)),
        (sk_ref, pl.ds(0, 1), 0, pl.ds(wide + cols, 2)),
        (sw_ref, pl.ds(1, 1), 0, pl.ds(wide + cols, 1)),
        (se_ref, pl.ds(1, 1), 0, pl.ds(wide + cols + 1, 1)),
        (ck_ref, pl.ds(0, 1), 0, pl.ds(2 * wide + cols, 2)),
        (cw_ref, pl.ds(1, 1), 0, pl.ds(2 * wide + cols, 1)),
        (ce_ref, pl.ds(1, 1), 0, pl.ds(2 * wide + cols + 1, 1)),
    )

    def copies(g):
        lanes = pl.ds(0, LANES) if g == 0 else pl.ds(LANES, width - LANES)
        return [
            pltpu.make_async_copy(
                ref.at[:, row, :, :, lanes], kv.at[part, place, :, lanes], sems.at[g, i]
            )
            for i, (ref, part, row, place) in enumerate(moves)
        ]

    pieces = range(min(groups, 2))
    for piece in pieces:
        for copy in copies(piece):
            copy.start()
    for b in range(cols):
        for part in range(2):
            grad[b, part, samples] = jnp.zeros((cells, LANES), jnp.float32)

    head = lax.broadcasted_iota(jnp.int32, (cells, LANES), 1) // HEAD_DIM
    masks = [head == h for h in range(GROUP)]

    def spread(rows):
        zero = jnp.zeros_like(rows)
        return jnp.concatenate([jnp.where(m, rows, zero) for m in masks], axis=0)

    def step(g):
        lanes = pl.ds(g * LANES, LANES)
        if g in pieces:
            for copy in copies(g):
                copy.wait()
        spans = range(cols)
        listed = [[slots[b, s] for s in range(samples)] for b in spans]
        query = [spread(q_ref[0, b, :, lanes]) for b in spans]
        upstream = [spread(c_ref[0, b, :, lanes]) for b in spans]
        keys = [jnp.concatenate([kv[0, s, :, lanes] for s in x], axis=0) for x in listed]
        values = [jnp.concatenate([kv[1, s, :, lanes] for s in x], axis=0) for x in listed]
        scores = [dot(keys[b], query[b], ((1,), (1,))) for b in spans]
        pressure = [dot(values[b], upstream[b], ((1,), (1,))) for b in spans]
        for b in spans:
            highest = jnp.max(scores[b], axis=0, keepdims=True)
            raised = jnp.exp2((scores[b] - highest) * (scale * LOG2E))
            weights = raised * (1.0 / jnp.sum(raised, axis=0, keepdims=True))
            weights_low = weights.astype(low)
            inner = jnp.sum(weights * pressure[b], axis=0, keepdims=True)
            score_grad = (weights * (pressure[b] - inner) * scale).astype(low)
            grad_values = dot(weights_low, upstream[b], ((1,), (0,)))
            grad_keys = dot(score_grad, query[b], ((1,), (0,)))
            shares[0, b, g] = score_grad
            shares[1, b, g] = weights_low
            for s in range(samples):
                grad[b, 0, s] = grad_keys[s * cells : (s + 1) * cells]
                grad[b, 1, s] = grad_values[s * cells : (s + 1) * cells]

        def merged(part, row, col):
            place = {cols: -1, cols + 1: cols}.get(col, col)
            slot = row * wide + col
            terms = [
                grad[b, part, places[b, slot]] for b in range(cols) if abs(b - place) <= 1
            ]
            return sum(terms[1:], terms[0])

        for c in range(cols):
            gik_ref[0, 0, c, :, lanes] = merged(0, 2, c).astype(low)
            giv_ref[0, 0, c, :, lanes] = merged(1, 2, c)
        for part in range(2):
            for c in range(cols):
                gown_ref[part, 0, c, :, lanes] = merged(part, 0, c)
            for c in range(wide):
                gintra_ref[part, 0, c, :, lanes] = merged(part, 1, c).astype(low)
        for side in range(2):
            gsk_ref[0, 0, side, :, lanes] = merged(0, 0, cols + side)
            gsv_ref[0, 0, side, :, lanes] = merged(1, 0, cols + side)
            gck_ref[0, 0, side, :, lanes] = merged(0, 2, cols + side).astype(low)
        gcw_ref[0, 0, 0, :, lanes] = merged(1, 2, cols).astype(low)
        gce_ref[0, 0, 0, :, lanes] = merged(1, 2, cols + 1).astype(low)

    for g in range(groups):
        step(g)


def attention(slots, places, operands):
    queries = operands[0]
    _, cols, cells, width = queries.shape
    wide = cols + 2
    samples = slots.shape[1]

    def out(lead, dtype):
        return jax.ShapeDtypeStruct(lead + (cells, width), dtype)

    low, full = jnp.bfloat16, jnp.float32
    keys = samples * cells
    outs = [
        out((2, 3 * wide), low),
        jax.ShapeDtypeStruct((2, cols, width // LANES, keys, LANES), low),
        out((2, 1, cols), full),
        out((1, 1, 2), full),
        out((1, 1, 2), full),
        out((2, 1, wide), low),
        out((1, 1, cols), low),
        out((1, 1, cols), full),
        out((1, 1, 2), low),
        out((1, 1, 1), low),
        out((1, 1, 1), low),
    ]
    flops = 2 * 4 * cols * width * GROUP * cells * keys
    moved = sum(x.size * x.dtype.itemsize for x in list(operands) + outs)
    scalar, vector, anywhere = (
        pl.BlockSpec(memory_space=space) for space in (pltpu.SMEM, pltpu.VMEM, pl.ANY)
    )
    return pl.pallas_call(
        attention_kernel,
        out_shape=outs,
        in_specs=[scalar] * 2 + [vector] * 2 + [anywhere] * (len(operands) - 2),
        out_specs=[vector] * len(outs),
        scratch_shapes=[
            pltpu.VMEM((cols, 2, samples + 1, cells, LANES), full),
            pltpu.SemaphoreType.DMA((2, len(operands) - 2)),
        ],
        cost_estimate=pl.CostEstimate(
            flops=flops, bytes_accessed=moved, transcendentals=cols * width * keys
        ),
        compiler_params=pltpu.CompilerParams(vmem_limit_bytes=20 * 1024 * 1024),
        name="attention",
    )(slots, places, *operands)


def stage_kernel(*refs):
    sems = refs[-1]
    count = len(refs) // 2
    copies = [
        pltpu.make_async_copy(refs[i], refs[count + i], sems.at[i]) for i in range(count)
    ]
    for copy in copies:
        copy.start()
    for copy in copies:
        copy.wait()


def stage(*arrays):
    return pl.pallas_call(
        stage_kernel,
        out_shape=[jax.ShapeDtypeStruct(x.shape, x.dtype) for x in arrays],
        in_specs=[pl.BlockSpec(memory_space=pl.ANY) for _ in arrays],
        out_specs=[pl.BlockSpec(memory_space=pltpu.VMEM) for _ in arrays],
        scratch_shapes=[pltpu.SemaphoreType.DMA((len(arrays),))],
        compiler_params=pltpu.CompilerParams(vmem_limit_bytes=8 * 1024 * 1024),
        name="stage",
    )(*arrays)


def finish_kernel(slots, kv, shares, gq_ref, att_ref):
    _, cols, cells, width = att_ref.shape
    samples = slots.shape[1]
    head = lax.broadcasted_iota(jnp.int32, (cells, LANES), 1) // HEAD_DIM
    for g in range(width // LANES):
        lanes = pl.ds(g * LANES, LANES)
        for b in range(cols):
            for part, ref in enumerate((gq_ref, att_ref)):
                rows = jnp.concatenate(
                    [kv[part, slots[b, s], :, lanes] for s in range(samples)], axis=0
                )
                sums = dot(shares[part, b, g], rows, ((0,), (0,)))
                out = sums[:cells]
                for h in range(1, GROUP):
                    out = jnp.where(head == h, sums[h * cells : (h + 1) * cells], out)
                ref[0, b, :, lanes] = out.astype(ref.dtype)


def finish(slots, kv, shares, like):
    scalar, vector = (pl.BlockSpec(memory_space=space) for space in (pltpu.SMEM, pltpu.VMEM))
    shape = jax.ShapeDtypeStruct(like.shape, like.dtype)
    return pl.pallas_call(
        finish_kernel,
        out_shape=[shape, shape],
        in_specs=[scalar, vector, vector],
        out_specs=[vector, vector],
        cost_estimate=pl.CostEstimate(
            flops=4 * shares.size * LANES, bytes_accessed=2 * shares.size, transcendentals=0
        ),
        compiler_params=pltpu.CompilerParams(vmem_limit_bytes=16 * 1024 * 1024),
        name="finish",
    )(slots, kv, shares)


def block_slots(blocks, cols):
    sectors = cols * lax.axis_size("lon")
    lat, lon = lax.axis_index("lat"), lax.axis_index("lon")
    down = blocks // sectors - lat
    near = jnp.where(lat % 2 == 0, 1, -1)
    row = jnp.where(down == 0, 0, jnp.where(down == near, 1, 2))
    place = (blocks % sectors - lon * cols + 1) % sectors
    col = jnp.where(place == 0, cols, jnp.where(place <= cols, place - 1, cols + 1))
    slots = row * (cols + 2) + col
    samples = blocks.shape[-1]
    listed = slots[:, :, None] == jnp.arange(3 * (cols + 2), dtype=jnp.int32)
    order = jnp.arange(samples, dtype=jnp.int32)[None, :, None]
    places = jnp.min(jnp.where(listed, order, samples), axis=1)
    return slots, places


def edges(first, last, cols):
    still = ((0, 0, 0),)
    return lax.pad(first, jnp.zeros((), first.dtype), still * 2 + ((0, cols - 1, 0),) + still * 2) + lax.pad(
        last, jnp.zeros((), last.dtype), still * 2 + ((cols - 1, 0, 0),) + still * 2
    )


def body(queries, keys_values, cotangent, blocks):
    cols = queries.shape[1]
    slots, places = block_slots(blocks[0], cols)

    keys, values = keys_values[:1], keys_values[1:]
    west_keys = lon_shift(keys[:, :, cols - 1 :], 1)
    east_keys = lon_shift(keys[:, :, :1], -1)
    west_values = lon_shift(values[:, :, cols - 1 :], 1)
    east_values = lon_shift(values[:, :, :1], -1)
    inter = inter_swap(keys_values)
    intra = intra_swap(keys_values)
    side_keys = jnp.concatenate([west_keys, east_keys], axis=2)
    corner_keys = inter_swap(side_keys)
    corner_west = lon_shift(inter[1:, :, cols - 1 :], 1)
    corner_east = lon_shift(inter[1:, :, :1], -1)
    intra_side_keys = intra_swap(side_keys)
    intra_west = intra_swap(west_values)
    intra_east = intra_swap(east_values)

    queries_near, cotangent_near, own_near = stage(queries, cotangent, keys_values)
    operands = (
        queries_near,
        cotangent_near,
        own_near,
        intra,
        inter,
        west_keys,
        east_keys,
        west_values,
        east_values,
        intra_side_keys,
        intra_west,
        intra_east,
        corner_keys,
        corner_west,
        corner_east,
    )
    outs = attention(slots, places, operands)
    kv, shares, own, side_k, side_v, to_intra, near_k, near_v, far_k, far_w, far_e = outs

    low, full = jnp.bfloat16, jnp.float32
    from_k = inter_swap(far_k)
    from_w = lon_shift(far_w, -1)
    from_e = lon_shift(far_e, 1)
    from_intra = intra_swap(to_intra)
    from_inter_k = inter_swap(near_k)
    side_v = (side_v + from_intra[1:, :, cols:].astype(full)).astype(low)
    from_east_v = lon_shift(side_v[:, :, :1], -1)
    from_west_v = lon_shift(side_v[:, :, 1:], 1)
    side_k = (side_k + from_intra[:1, :, cols:].astype(full) + from_k.astype(full)).astype(low)
    from_east_k = lon_shift(side_k[:, :, :1], -1)
    from_west_k = lon_shift(side_k[:, :, 1:], 1)
    near_v = (near_v + edges(from_e.astype(full), from_w.astype(full), cols)).astype(low)
    from_inter_v = inter_swap(near_v)

    grad_queries, attended = finish(slots, kv, shares, queries)

    def total(part, inter, first, last):
        piece = own[part : part + 1] + from_intra[part : part + 1, :, :cols].astype(full)
        piece = piece + inter.astype(full) + edges(first.astype(full), last.astype(full), cols)
        return piece.astype(low)

    grads = jnp.concatenate(
        [
            total(0, from_inter_k, from_west_k, from_east_k),
            total(1, from_inter_v, from_west_v, from_east_v),
        ],
        axis=0,
    )
    return (attended, grad_queries, grads)


def solution(mesh):
    placed = (
        P("lat", "lon", None, None),
        P(None, "lat", "lon", None, None),
        P("lat", "lon", None, None),
        P("lat", "lon", None),
    )
    return jax.shard_map(
        body,
        mesh=mesh,
        in_specs=placed,
        out_specs=(placed[0], placed[0], placed[1]),
        check_vma=False,
    )
```

```python
import jax
import jax.numpy as jnp
from jax import lax
from jax.experimental import pallas as pl
from jax.experimental.pallas import tpu as pltpu
from jax.sharding import PartitionSpec as P


HEAD_DIM = 64
GROUP = 4
LANES = GROUP * HEAD_DIM
LOG2E = 1.4426950408889634


def lon_shift(value, steps):
    count = lax.axis_size("lon")
    return lax.ppermute(value, "lon", [(i, (i + steps) % count) for i in range(count)])


def intra_swap(value):
    count = lax.axis_size("lat")
    return lax.ppermute(value, "lat", [(i, i ^ 1) for i in range(count) if i ^ 1 < count])


def inter_swap(value):
    count = lax.axis_size("lat")
    pairs = [(i, i + 1 if i % 2 else i - 1) for i in range(count)]
    return lax.ppermute(value, "lat", [(i, j) for i, j in pairs if 0 <= j < count])


def dot(a, b, dims):
    return lax.dot_general(a, b, (dims, ((), ())), preferred_element_type=jnp.float32)


def attention_kernel(
    slots,
    places,
    qc_ref,
    fk_ref,
    lk_ref,
    fv_ref,
    lv_ref,
    intra_ref,
    inter_ref,
    wk_ref,
    ek_ref,
    wv_ref,
    ev_ref,
    sk_ref,
    sw_ref,
    se_ref,
    ck_ref,
    cw_ref,
    ce_ref,
    kv,
    shares,
    gown_ref,
    gsk_ref,
    gsv_ref,
    gintra_ref,
    gik_ref,
    giv_ref,
    gck_ref,
    gcw_ref,
    gce_ref,
    grad,
    sems,
):
    _, cols, cells, width = qc_ref.shape
    wide = cols + 2
    samples = slots.shape[1]
    groups = width // LANES
    scale = HEAD_DIM**-0.5
    low = jnp.bfloat16

    far = pl.ds(2 * wide, cols)
    moves = (
        (fk_ref, pl.ds(0, 1), 0, pl.ds(0, cols - 1)),
        (lk_ref, pl.ds(0, 1), 0, pl.ds(cols - 1, 1)),
        (fv_ref, pl.ds(1, 1), 0, pl.ds(0, cols - 1)),
        (lv_ref, pl.ds(1, 1), 0, pl.ds(cols - 1, 1)),
        (intra_ref, slice(None), 0, pl.ds(wide, cols)),
        (inter_ref, slice(None), 0, far),
        (wk_ref, pl.ds(0, 1), 0, pl.ds(cols, 1)),
        (ek_ref, pl.ds(0, 1), 0, pl.ds(cols + 1, 1)),
        (wv_ref, pl.ds(1, 1), 0, pl.ds(cols, 1)),
        (ev_ref, pl.ds(1, 1), 0, pl.ds(cols + 1, 1)),
        (sk_ref, pl.ds(0, 1), 0, pl.ds(wide + cols, 2)),
        (sw_ref, pl.ds(1, 1), 0, pl.ds(wide + cols, 1)),
        (se_ref, pl.ds(1, 1), 0, pl.ds(wide + cols + 1, 1)),
        (ck_ref, pl.ds(0, 1), 0, pl.ds(2 * wide + cols, 2)),
        (cw_ref, pl.ds(1, 1), 0, pl.ds(2 * wide + cols, 1)),
        (ce_ref, pl.ds(1, 1), 0, pl.ds(2 * wide + cols + 1, 1)),
    )

    def copies(g):
        lanes = pl.ds(0, LANES) if g == 0 else pl.ds(LANES, width - LANES)
        return [
            pltpu.make_async_copy(
                ref.at[:, row, :, :, lanes], kv.at[part, place, :, lanes], sems.at[g, i]
            )
            for i, (ref, part, row, place) in enumerate(moves)
        ]

    pieces = range(min(groups, 2))
    for piece in pieces:
        for copy in copies(piece):
            copy.start()
    for b in range(cols):
        for part in range(2):
            grad[b, part, samples] = jnp.zeros((cells, LANES), jnp.float32)

    head = lax.broadcasted_iota(jnp.int32, (cells, LANES), 1) // HEAD_DIM
    masks = [head == h for h in range(GROUP)]

    def spread(rows):
        zero = jnp.zeros_like(rows)
        return jnp.concatenate([jnp.where(m, rows, zero) for m in masks], axis=0)

    def step(g):
        lanes = pl.ds(g * LANES, LANES)
        if g in pieces:
            for copy in copies(g):
                copy.wait()
        spans = range(cols)
        listed = [[slots[b, s] for s in range(samples)] for b in spans]
        query = [spread(qc_ref[0, b, :, lanes]) for b in spans]
        upstream = [spread(qc_ref[1, b, :, lanes]) for b in spans]
        keys = [jnp.concatenate([kv[0, s, :, lanes] for s in x], axis=0) for x in listed]
        values = [jnp.concatenate([kv[1, s, :, lanes] for s in x], axis=0) for x in listed]
        scores = [dot(keys[b], query[b], ((1,), (1,))) for b in spans]
        pressure = [dot(values[b], upstream[b], ((1,), (1,))) for b in spans]
        for b in spans:
            highest = jnp.max(scores[b], axis=0, keepdims=True)
            raised = jnp.exp2((scores[b] - highest) * (scale * LOG2E))
            weights = raised * (1.0 / jnp.sum(raised, axis=0, keepdims=True))
            weights_low = weights.astype(low)
            inner = jnp.sum(weights * pressure[b], axis=0, keepdims=True)
            score_grad = (weights * (pressure[b] - inner) * scale).astype(low)
            grad_values = dot(weights_low, upstream[b], ((1,), (0,)))
            grad_keys = dot(score_grad, query[b], ((1,), (0,)))
            shares[0, b, g] = score_grad
            shares[1, b, g] = weights_low
            for s in range(samples):
                grad[b, 0, s] = grad_keys[s * cells : (s + 1) * cells]
                grad[b, 1, s] = grad_values[s * cells : (s + 1) * cells]

        def merged(part, row, col):
            place = {cols: -1, cols + 1: cols}.get(col, col)
            slot = row * wide + col
            terms = [
                grad[b, part, places[b, slot]] for b in range(cols) if abs(b - place) <= 1
            ]
            return sum(terms[1:], terms[0])

        for c in range(cols):
            gik_ref[0, 0, c, :, lanes] = merged(0, 2, c).astype(low)
            giv_ref[0, 0, c, :, lanes] = merged(1, 2, c)
        for part in range(2):
            for c in range(cols):
                gown_ref[part, 0, c, :, lanes] = merged(part, 0, c)
            for c in range(wide):
                gintra_ref[part, 0, c, :, lanes] = merged(part, 1, c).astype(low)
        for side in range(2):
            gsk_ref[0, 0, side, :, lanes] = merged(0, 0, cols + side)
            gsv_ref[0, 0, side, :, lanes] = merged(1, 0, cols + side)
            gck_ref[0, 0, side, :, lanes] = merged(0, 2, cols + side).astype(low)
        gcw_ref[0, 0, 0, :, lanes] = merged(1, 2, cols).astype(low)
        gce_ref[0, 0, 0, :, lanes] = merged(1, 2, cols + 1).astype(low)

    for g in range(groups):
        step(g)


def attention(slots, places, operands):
    _, cols, cells, width = operands[0].shape
    wide = cols + 2
    samples = slots.shape[1]

    def out(lead, dtype):
        return jax.ShapeDtypeStruct(lead + (cells, width), dtype)

    low, full = jnp.bfloat16, jnp.float32
    keys = samples * cells
    outs = [
        out((2, 3 * wide), low),
        jax.ShapeDtypeStruct((2, cols, width // LANES, keys, LANES), low),
        out((2, 1, cols), full),
        out((1, 1, 2), full),
        out((1, 1, 2), full),
        out((2, 1, wide), low),
        out((1, 1, cols), low),
        out((1, 1, cols), full),
        out((1, 1, 2), low),
        out((1, 1, 1), low),
        out((1, 1, 1), low),
    ]
    flops = 2 * 4 * cols * width * GROUP * cells * keys
    moved = sum(x.size * x.dtype.itemsize for x in list(operands) + outs)
    scalar, vector, anywhere = (
        pl.BlockSpec(memory_space=space) for space in (pltpu.SMEM, pltpu.VMEM, pl.ANY)
    )
    return pl.pallas_call(
        attention_kernel,
        out_shape=outs,
        in_specs=[scalar] * 2 + [vector] + [anywhere] * (len(operands) - 1),
        out_specs=[vector] * len(outs),
        scratch_shapes=[
            pltpu.VMEM((cols, 2, samples + 1, cells, LANES), full),
            pltpu.SemaphoreType.DMA((2, len(operands) - 1)),
        ],
        cost_estimate=pl.CostEstimate(
            flops=flops, bytes_accessed=moved, transcendentals=cols * width * keys
        ),
        compiler_params=pltpu.CompilerParams(vmem_limit_bytes=20 * 1024 * 1024),
        name="attention",
    )(slots, places, *operands)


def finish_kernel(slots, kv, shares, gq_ref, att_ref):
    _, cols, cells, width = att_ref.shape
    samples = slots.shape[1]
    head = lax.broadcasted_iota(jnp.int32, (cells, LANES), 1) // HEAD_DIM
    for g in range(width // LANES):
        lanes = pl.ds(g * LANES, LANES)
        for b in range(cols):
            for part, ref in enumerate((gq_ref, att_ref)):
                rows = jnp.concatenate(
                    [kv[part, slots[b, s], :, lanes] for s in range(samples)], axis=0
                )
                sums = dot(shares[part, b, g], rows, ((0,), (0,)))
                out = sums[:cells]
                for h in range(1, GROUP):
                    out = jnp.where(head == h, sums[h * cells : (h + 1) * cells], out)
                ref[0, b, :, lanes] = out.astype(ref.dtype)


def finish(slots, kv, shares, like):
    scalar, vector = (pl.BlockSpec(memory_space=space) for space in (pltpu.SMEM, pltpu.VMEM))
    shape = jax.ShapeDtypeStruct(like.shape, like.dtype)
    return pl.pallas_call(
        finish_kernel,
        out_shape=[shape, shape],
        in_specs=[scalar, vector, vector],
        out_specs=[vector, vector],
        cost_estimate=pl.CostEstimate(
            flops=4 * shares.size * LANES, bytes_accessed=2 * shares.size, transcendentals=0
        ),
        compiler_params=pltpu.CompilerParams(vmem_limit_bytes=16 * 1024 * 1024),
        name="finish",
    )(slots, kv, shares)


def block_slots(blocks, cols):
    sectors = cols * lax.axis_size("lon")
    lat, lon = lax.axis_index("lat"), lax.axis_index("lon")
    down = blocks // sectors - lat
    near = jnp.where(lat % 2 == 0, 1, -1)
    row = jnp.where(down == 0, 0, jnp.where(down == near, 1, 2))
    place = (blocks % sectors - lon * cols + 1) % sectors
    col = jnp.where(place == 0, cols, jnp.where(place <= cols, place - 1, cols + 1))
    slots = row * (cols + 2) + col
    samples = blocks.shape[-1]
    listed = slots[:, :, None] == jnp.arange(3 * (cols + 2), dtype=jnp.int32)
    order = jnp.arange(samples, dtype=jnp.int32)[None, :, None]
    places = jnp.min(jnp.where(listed, order, samples), axis=1)
    return slots, places


def edges(first, last, cols):
    still = ((0, 0, 0),)
    return lax.pad(first, jnp.zeros((), first.dtype), still * 2 + ((0, cols - 1, 0),) + still * 2) + lax.pad(
        last, jnp.zeros((), last.dtype), still * 2 + ((cols - 1, 0, 0),) + still * 2
    )


def body(queries, keys_values, cotangent, blocks):
    cols = queries.shape[1]
    slots, places = block_slots(blocks[0], cols)

    keys, values = keys_values[:1], keys_values[1:]
    west_keys = lon_shift(keys[:, :, cols - 1 :], 1)
    east_keys = lon_shift(keys[:, :, :1], -1)
    west_values = lon_shift(values[:, :, cols - 1 :], 1)
    east_values = lon_shift(values[:, :, :1], -1)
    inter = inter_swap(keys_values)
    intra = intra_swap(keys_values)
    side_keys = jnp.concatenate([west_keys, east_keys], axis=2)
    corner_keys = inter_swap(side_keys)
    corner_west = lon_shift(inter[1:, :, cols - 1 :], 1)
    corner_east = lon_shift(inter[1:, :, :1], -1)
    intra_side_keys = intra_swap(side_keys)
    intra_west = intra_swap(west_values)
    intra_east = intra_swap(east_values)

    queries_cotangent = jnp.concatenate([queries, cotangent], axis=0)
    operands = (
        queries_cotangent,
        keys[:, :, : cols - 1],
        keys[:, :, cols - 1 :],
        values[:, :, : cols - 1],
        values[:, :, cols - 1 :],
        intra,
        inter,
        west_keys,
        east_keys,
        west_values,
        east_values,
        intra_side_keys,
        intra_west,
        intra_east,
        corner_keys,
        corner_west,
        corner_east,
    )
    outs = attention(slots, places, operands)
    kv, shares, own, side_k, side_v, to_intra, near_k, near_v, far_k, far_w, far_e = outs

    low, full = jnp.bfloat16, jnp.float32
    from_k = inter_swap(far_k)
    from_w = lon_shift(far_w, -1)
    from_e = lon_shift(far_e, 1)
    from_intra = intra_swap(to_intra)
    from_inter_k = inter_swap(near_k)
    side_v = (side_v + from_intra[1:, :, cols:].astype(full)).astype(low)
    side_k = (side_k + from_intra[:1, :, cols:].astype(full) + from_k.astype(full)).astype(low)
    to_east = jnp.concatenate([side_k[:, :, :1], side_v[:, :, :1]], axis=0)
    to_west = jnp.concatenate([side_k[:, :, 1:], side_v[:, :, 1:]], axis=0)
    from_east = lon_shift(to_east, -1)
    from_west = lon_shift(to_west, 1)
    from_east_k, from_east_v = from_east[:1], from_east[1:]
    from_west_k, from_west_v = from_west[:1], from_west[1:]
    near_v = (near_v + edges(from_e.astype(full), from_w.astype(full), cols)).astype(low)
    from_inter_v = inter_swap(near_v)

    grad_queries, attended = finish(slots, kv, shares, queries)

    def total(part, inter, first, last):
        piece = own[part : part + 1] + from_intra[part : part + 1, :, :cols].astype(full)
        piece = piece + inter.astype(full) + edges(first.astype(full), last.astype(full), cols)
        return piece.astype(low)

    grads = jnp.concatenate(
        [
            total(0, from_inter_k, from_west_k, from_east_k),
            total(1, from_inter_v, from_west_v, from_east_v),
        ],
        axis=0,
    )
    return (attended, grad_queries, grads)


def solution(mesh):
    placed = (
        P("lat", "lon", None, None),
        P(None, "lat", "lon", None, None),
        P("lat", "lon", None, None),
        P("lat", "lon", None),
    )
    return jax.shard_map(
        body,
        mesh=mesh,
        in_specs=placed,
        out_specs=(placed[0], placed[0], placed[1]),
        check_vma=False,
    )
```

```python
import jax
import jax.numpy as jnp
from jax import lax
from jax.experimental import pallas as pl
from jax.experimental.pallas import tpu as pltpu
from jax.sharding import PartitionSpec as P


HEAD_DIM = 64
GROUP = 4
LANES = GROUP * HEAD_DIM
LOG2E = 1.4426950408889634


def lon_shift(value, steps):
    count = lax.axis_size("lon")
    return lax.ppermute(value, "lon", [(i, (i + steps) % count) for i in range(count)])


def intra_swap(value):
    count = lax.axis_size("lat")
    return lax.ppermute(value, "lat", [(i, i ^ 1) for i in range(count) if i ^ 1 < count])


def inter_swap(value):
    count = lax.axis_size("lat")
    pairs = [(i, i + 1 if i % 2 else i - 1) for i in range(count)]
    return lax.ppermute(value, "lat", [(i, j) for i, j in pairs if 0 <= j < count])


def dot(a, b, dims):
    return lax.dot_general(a, b, (dims, ((), ())), preferred_element_type=jnp.float32)


def attention_kernel(
    slots,
    places,
    qc_ref,
    fk_ref,
    lk_ref,
    fv_ref,
    lv_ref,
    intra_ref,
    inter_ref,
    wk_ref,
    ek_ref,
    wv_ref,
    ev_ref,
    sk_ref,
    sw_ref,
    se_ref,
    ck_ref,
    cw_ref,
    ce_ref,
    kv,
    shares,
    gown_ref,
    gsk_ref,
    gsv_ref,
    gintra_ref,
    gik_ref,
    giv_ref,
    gck_ref,
    gcw_ref,
    gce_ref,
    grad,
    sems,
):
    _, cols, cells, width = qc_ref.shape
    wide = cols + 2
    samples = slots.shape[1]
    groups = width // LANES
    scale = HEAD_DIM**-0.5
    low = jnp.bfloat16

    far = pl.ds(2 * wide, cols)
    moves = (
        (fk_ref, pl.ds(0, 1), 0, pl.ds(0, cols - 1)),
        (lk_ref, pl.ds(0, 1), 0, pl.ds(cols - 1, 1)),
        (fv_ref, pl.ds(1, 1), 0, pl.ds(0, cols - 1)),
        (lv_ref, pl.ds(1, 1), 0, pl.ds(cols - 1, 1)),
        (intra_ref, slice(None), 0, pl.ds(wide, cols)),
        (inter_ref, slice(None), 0, far),
        (wk_ref, pl.ds(0, 1), 0, pl.ds(cols, 1)),
        (ek_ref, pl.ds(0, 1), 0, pl.ds(cols + 1, 1)),
        (wv_ref, pl.ds(1, 1), 0, pl.ds(cols, 1)),
        (ev_ref, pl.ds(1, 1), 0, pl.ds(cols + 1, 1)),
        (sk_ref, pl.ds(0, 1), 0, pl.ds(wide + cols, 2)),
        (sw_ref, pl.ds(1, 1), 0, pl.ds(wide + cols, 1)),
        (se_ref, pl.ds(1, 1), 0, pl.ds(wide + cols + 1, 1)),
        (ck_ref, pl.ds(0, 1), 0, pl.ds(2 * wide + cols, 2)),
        (cw_ref, pl.ds(1, 1), 0, pl.ds(2 * wide + cols, 1)),
        (ce_ref, pl.ds(1, 1), 0, pl.ds(2 * wide + cols + 1, 1)),
    )

    def copies(g):
        lanes = pl.ds(0, LANES) if g == 0 else pl.ds(LANES, width - LANES)
        return [
            pltpu.make_async_copy(
                ref.at[:, row, :, :, lanes], kv.at[part, place, :, lanes], sems.at[g, i]
            )
            for i, (ref, part, row, place) in enumerate(moves)
        ]

    pieces = range(min(groups, 2))
    for piece in pieces:
        for copy in copies(piece):
            copy.start()
    for b in range(cols):
        for part in range(2):
            grad[b, part, samples] = jnp.zeros((cells, LANES), jnp.float32)

    head = lax.broadcasted_iota(jnp.int32, (cells, LANES), 1) // HEAD_DIM
    masks = [head == h for h in range(GROUP)]

    def spread(rows):
        zero = jnp.zeros_like(rows)
        return jnp.concatenate([jnp.where(m, rows, zero) for m in masks], axis=0)

    def step(g):
        lanes = pl.ds(g * LANES, LANES)
        if g in pieces:
            for copy in copies(g):
                copy.wait()
        spans = range(cols)
        listed = [[slots[b, s] for s in range(samples)] for b in spans]
        query = [spread(qc_ref[0, b, :, lanes]) for b in spans]
        upstream = [spread(qc_ref[1, b, :, lanes]) for b in spans]
        keys = [jnp.concatenate([kv[0, s, :, lanes] for s in x], axis=0) for x in listed]
        values = [jnp.concatenate([kv[1, s, :, lanes] for s in x], axis=0) for x in listed]
        scores = [dot(keys[b], query[b], ((1,), (1,))) for b in spans]
        pressure = [dot(values[b], upstream[b], ((1,), (1,))) for b in spans]
        for b in spans:
            highest = jnp.max(scores[b], axis=0, keepdims=True)
            raised = jnp.exp2((scores[b] - highest) * (scale * LOG2E))
            weights = raised * (1.0 / jnp.sum(raised, axis=0, keepdims=True))
            weights_low = weights.astype(low)
            inner = jnp.sum(weights * pressure[b], axis=0, keepdims=True)
            score_grad = (weights * (pressure[b] - inner) * scale).astype(low)
            grad_values = dot(weights_low, upstream[b], ((1,), (0,)))
            grad_keys = dot(score_grad, query[b], ((1,), (0,)))
            shares[0, b, g] = score_grad
            shares[1, b, g] = weights_low
            for s in range(samples):
                grad[b, 0, s] = grad_keys[s * cells : (s + 1) * cells]
                grad[b, 1, s] = grad_values[s * cells : (s + 1) * cells]

        def merged(part, row, col):
            place = {cols: -1, cols + 1: cols}.get(col, col)
            slot = row * wide + col
            terms = [
                grad[b, part, places[b, slot]] for b in range(cols) if abs(b - place) <= 1
            ]
            return sum(terms[1:], terms[0])

        for c in range(cols):
            gik_ref[0, 0, c, :, lanes] = merged(0, 2, c).astype(low)
            giv_ref[0, 0, c, :, lanes] = merged(1, 2, c)
        for part in range(2):
            for c in range(cols):
                gown_ref[part, 0, c, :, lanes] = merged(part, 0, c)
            for c in range(wide):
                gintra_ref[part, 0, c, :, lanes] = merged(part, 1, c).astype(low)
        for side in range(2):
            gsk_ref[0, 0, side, :, lanes] = merged(0, 0, cols + side)
            gsv_ref[0, 0, side, :, lanes] = merged(1, 0, cols + side)
            gck_ref[0, 0, side, :, lanes] = merged(0, 2, cols + side).astype(low)
        gcw_ref[0, 0, 0, :, lanes] = merged(1, 2, cols).astype(low)
        gce_ref[0, 0, 0, :, lanes] = merged(1, 2, cols + 1).astype(low)

    for g in range(groups):
        step(g)


def attention(slots, places, operands):
    _, cols, cells, width = operands[0].shape
    wide = cols + 2
    samples = slots.shape[1]

    def out(lead, dtype):
        return jax.ShapeDtypeStruct(lead + (cells, width), dtype)

    low, full = jnp.bfloat16, jnp.float32
    keys = samples * cells
    outs = [
        out((2, 3 * wide), low),
        jax.ShapeDtypeStruct((2, cols, width // LANES, keys, LANES), low),
        out((2, 1, cols), full),
        out((1, 1, 2), full),
        out((1, 1, 2), full),
        out((2, 1, wide), low),
        out((1, 1, cols), low),
        out((1, 1, cols), full),
        out((1, 1, 2), low),
        out((1, 1, 1), low),
        out((1, 1, 1), low),
    ]
    flops = 2 * 4 * cols * width * GROUP * cells * keys
    moved = sum(x.size * x.dtype.itemsize for x in list(operands) + outs)
    scalar, vector, anywhere = (
        pl.BlockSpec(memory_space=space) for space in (pltpu.SMEM, pltpu.VMEM, pl.ANY)
    )
    return pl.pallas_call(
        attention_kernel,
        out_shape=outs,
        in_specs=[scalar] * 2 + [vector] + [anywhere] * (len(operands) - 1),
        out_specs=[vector] * len(outs),
        scratch_shapes=[
            pltpu.VMEM((cols, 2, samples + 1, cells, LANES), full),
            pltpu.SemaphoreType.DMA((2, len(operands) - 1)),
        ],
        cost_estimate=pl.CostEstimate(
            flops=flops, bytes_accessed=moved, transcendentals=cols * width * keys
        ),
        compiler_params=pltpu.CompilerParams(vmem_limit_bytes=20 * 1024 * 1024),
        name="attention",
    )(slots, places, *operands)


def finish_kernel(slots, kv, shares, gq_ref, att_ref):
    _, cols, cells, width = att_ref.shape
    samples = slots.shape[1]
    head = lax.broadcasted_iota(jnp.int32, (cells, LANES), 1) // HEAD_DIM
    for g in range(width // LANES):
        lanes = pl.ds(g * LANES, LANES)
        for b in range(cols):
            for part, ref in enumerate((gq_ref, att_ref)):
                rows = jnp.concatenate(
                    [kv[part, slots[b, s], :, lanes] for s in range(samples)], axis=0
                )
                sums = dot(shares[part, b, g], rows, ((0,), (0,)))
                out = sums[:cells]
                for h in range(1, GROUP):
                    out = jnp.where(head == h, sums[h * cells : (h + 1) * cells], out)
                ref[0, b, :, lanes] = out.astype(ref.dtype)


def finish(slots, kv, shares, like):
    scalar, vector = (pl.BlockSpec(memory_space=space) for space in (pltpu.SMEM, pltpu.VMEM))
    shape = jax.ShapeDtypeStruct(like.shape, like.dtype)
    return pl.pallas_call(
        finish_kernel,
        out_shape=[shape, shape],
        in_specs=[scalar, vector, vector],
        out_specs=[vector, vector],
        cost_estimate=pl.CostEstimate(
            flops=4 * shares.size * LANES, bytes_accessed=2 * shares.size, transcendentals=0
        ),
        compiler_params=pltpu.CompilerParams(vmem_limit_bytes=16 * 1024 * 1024),
        name="finish",
    )(slots, kv, shares)


def block_slots(blocks, cols):
    sectors = cols * lax.axis_size("lon")
    lat, lon = lax.axis_index("lat"), lax.axis_index("lon")
    down = blocks // sectors - lat
    near = jnp.where(lat % 2 == 0, 1, -1)
    row = jnp.where(down == 0, 0, jnp.where(down == near, 1, 2))
    place = (blocks % sectors - lon * cols + 1) % sectors
    col = jnp.where(place == 0, cols, jnp.where(place <= cols, place - 1, cols + 1))
    slots = row * (cols + 2) + col
    samples = blocks.shape[-1]
    listed = slots[:, :, None] == jnp.arange(3 * (cols + 2), dtype=jnp.int32)
    order = jnp.arange(samples, dtype=jnp.int32)[None, :, None]
    places = jnp.min(jnp.where(listed, order, samples), axis=1)
    return slots, places


def edges(first, last, cols):
    still = ((0, 0, 0),)
    return lax.pad(first, jnp.zeros((), first.dtype), still * 2 + ((0, cols - 1, 0),) + still * 2) + lax.pad(
        last, jnp.zeros((), last.dtype), still * 2 + ((cols - 1, 0, 0),) + still * 2
    )


def body(queries, keys_values, cotangent, blocks):
    cols = queries.shape[1]
    slots, places = block_slots(blocks[0], cols)

    keys, values = keys_values[:1], keys_values[1:]
    west_keys = lon_shift(keys[:, :, cols - 1 :], 1)
    east_keys = lon_shift(keys[:, :, :1], -1)
    west_values = lon_shift(values[:, :, cols - 1 :], 1)
    east_values = lon_shift(values[:, :, :1], -1)
    inter = inter_swap(keys_values)
    intra = intra_swap(keys_values)
    side_keys = jnp.concatenate([west_keys, east_keys], axis=2)
    corner_keys = inter_swap(side_keys)
    corner_west = lon_shift(inter[1:, :, cols - 1 :], 1)
    corner_east = lon_shift(inter[1:, :, :1], -1)
    intra_side_keys = intra_swap(side_keys)
    intra_west = intra_swap(west_values)
    intra_east = intra_swap(east_values)

    queries_cotangent = jnp.concatenate([queries, cotangent], axis=0)
    operands = (
        queries_cotangent,
        keys[:, :, : cols - 1],
        keys[:, :, cols - 1 :],
        values[:, :, : cols - 1],
        values[:, :, cols - 1 :],
        intra,
        inter,
        west_keys,
        east_keys,
        west_values,
        east_values,
        intra_side_keys,
        intra_west,
        intra_east,
        corner_keys,
        corner_west,
        corner_east,
    )
    outs = attention(slots, places, operands)
    kv, shares, own, side_k, side_v, to_intra, near_k, near_v, far_k, far_w, far_e = outs

    low, full = jnp.bfloat16, jnp.float32
    from_k = inter_swap(far_k)
    from_w = lon_shift(far_w, -1)
    from_e = lon_shift(far_e, 1)
    from_intra = intra_swap(to_intra)
    from_inter_k = inter_swap(near_k)
    side_v = (side_v + from_intra[1:, :, cols:].astype(full)).astype(low)
    side_k = (side_k + from_intra[:1, :, cols:].astype(full) + from_k.astype(full)).astype(low)
    to_east = jnp.concatenate([side_k[:, :, :1], side_v[:, :, :1]], axis=0)
    to_west = jnp.concatenate([side_k[:, :, 1:], side_v[:, :, 1:]], axis=0)
    from_east = lon_shift(to_east, -1)
    from_west = lon_shift(to_west, 1)
    near_v = (near_v + edges(from_e.astype(full), from_w.astype(full), cols)).astype(low)
    from_inter_v = inter_swap(near_v)

    grad_queries, attended = finish(slots, kv, shares, queries)

    still = ((0, 0, 0),) * 4
    zero = jnp.zeros((), full)
    grads = own + from_intra[:, :, :cols].astype(full)
    grads = grads + lax.pad(from_inter_k.astype(full), zero, ((0, 1, 0),) + still)
    grads = grads + lax.pad(from_inter_v.astype(full), zero, ((1, 0, 0),) + still)
    grads = grads + edges(from_west.astype(full), from_east.astype(full), cols)
    grads = grads.astype(low)
    return (attended, grad_queries, grads)


def solution(mesh):
    placed = (
        P("lat", "lon", None, None),
        P(None, "lat", "lon", None, None),
        P("lat", "lon", None, None),
        P("lat", "lon", None),
    )
    return jax.shard_map(
        body,
        mesh=mesh,
        in_specs=placed,
        out_specs=(placed[0], placed[0], placed[1]),
        check_vma=False,
    )
```
